32 devices in a mesh: blk: 16 (over z, x, core), head: 2 (over y).
Axes of the slice: x: 2, y: 2, z: 4, core: 2. Of those that a mesh axis runs over, the one named last changes fastest.
Arguments:
- query: bfloat16 [4096, 4096], P(('blk', 'head')), may hold values from -128 to 128
- key: bfloat16 [2048, 4096], P('blk', 'head'), may hold values from -8 to 8
- value: bfloat16 [2048, 4096], P('blk', 'head'), may hold values from -6 to 6
- d_out: bfloat16 [4096, 4096], P(('blk', 'head')), may hold values from -6 to 6
- seg_map: int32 [32], replicated, may hold values from 0 to 7, never falling along the last dimension, each value on 1 to 8 neighbouring positions
- spans: int32 [8, 8], replicated, may hold values from 0 to 15, all different within a row
Outputs:
- attn_out: bfloat16 [4096, 4096], P(('blk', 'head'))
- d_query: bfloat16 [4096, 4096], P(('blk', 'head'))
- d_key: bfloat16 [2048, 4096], P('blk', 'head')
- d_value: bfloat16 [2048, 4096], P('blk', 'head')
The draws below stay inside these ranges and needn't reach their ends.
Inputs may be any that keep to these rules, and one draw needn't show every extreme that they name: `seg_map`: segment numbers never fall from one CAD block to the next; each segment covers 1 to 8 blocks, one exactly 8. `spans`: each row names 8 different document blocks; every document block is named by some row.
All inputs are finite; a program needn't handle non-finite values.
Results may differ from the reference program's by a relative error of at most 0.024.
Values may be sent and summed in bfloat16 or wider, within the bound.
A program may use at most 128 MiB of HBM per device.

```python
import math
import jax
import jax.numpy as jnp
import numpy as np
from jax import lax

HEADS = 32
HEAD_DIM = 128
BLOCK = 128
SPANS = 8
CAD_TOK = 4096
DOC_TOK = 2048
ROWS_GROUP = 256
CAD_BLOCKS = 32
DOC_BLOCKS = 16
SEGS = 8
N_BLK = 16


def draw_query(key, part):
    sample = jax.random.normal(jax.random.fold_in(key, 1), (CAD_TOK, HEADS * HEAD_DIM), jnp.float32)
    sample = jnp.clip(sample, -6.0, 6.0)
    return sample.astype(jnp.bfloat16)


def draw_key(key, part):
    sample = jax.random.normal(jax.random.fold_in(key, 2), (DOC_TOK, HEADS * HEAD_DIM), jnp.float32)
    sample = jnp.clip(sample, -6.0, 6.0)
    return sample.astype(jnp.bfloat16)


def level_of(rng, dims, shards, low, largest):
    level, own = 1.0, jax.random.fold_in(rng, 6)
    for dim, blocks in shards:
        heights = jnp.exp(jax.random.uniform(jax.random.fold_in(own, dim), (blocks,), jnp.float32, low / len(shards), largest / len(shards)))
        level = level * jnp.repeat(heights, dims[dim] // blocks).reshape([-1 if axis == dim else 1 for axis in range(len(dims))])
    return level


def picks_of(own_key, rows, amount, top, lift):
    order = jax.random.permutation(jax.random.fold_in(own_key, 1), amount)
    boost = order
    for power in range(3):
        boost = boost * boost // amount
    boost = boost * lift // amount
    chance = jax.random.randint(jax.random.fold_in(own_key, 2), (rows, amount), 0, 4096) + boost
    fixed_rows = jax.random.permutation(jax.random.fold_in(own_key, 3), rows)[jnp.arange(amount) % rows]
    chance = jnp.where(jnp.arange(rows)[:, None] == fixed_rows[None, :], 1 << 14, chance)
    score = chance * amount + jnp.arange(amount)
    return lax.top_k(score.astype(jnp.int32), top)[1].astype(jnp.int32)


def split_up(amount, total, most, slope):
    portions = [(1 << 20) // math.isqrt(grade ** slope) + 1 for grade in range(2, amount + 1)]
    surplus, counts = total - most - (amount - 1), [1] * (amount - 1)
    while surplus > 0:
        candidates = [i for i in range(amount - 1) if counts[i] < most]
        mass, left = sum([portions[i] for i in candidates]), surplus
        for i in candidates:
            extra = min(most - counts[i], max(1, left * portions[i] // mass), surplus)
            counts[i] = counts[i] + extra
            surplus = surplus - extra
    return np.array([most] + counts)


def uneven(rng, number_of, total, most, skew):
    if number_of == 2:
        one = jax.random.randint(rng, (), max(1, total - most), min(most, total - 1) + 1)
        return jnp.stack([one, total - one])
    lengths = jnp.asarray(split_up(number_of, total, most, skew), jnp.int32)
    pairs = (number_of - 1) // 2
    source_of, taker = lengths[1:1 + 2 * pairs:2], lengths[2:2 + 2 * pairs:2]
    slack = jnp.minimum(source_of - 1, most - taker)
    moved = jax.random.randint(jax.random.fold_in(rng, 1), (pairs,), 0, 1 << 20) % (slack + 1)
    lengths = lengths.at[1:1 + 2 * pairs:2].set(source_of - moved).at[2:2 + 2 * pairs:2].set(taker + moved)
    return lengths[jax.random.permutation(jax.random.fold_in(rng, 2), number_of)]


def scatter_about(key, extent, scale, limit, shards=(), kind=jnp.bfloat16):
    loudness = level_of(key, extent, shards, -0.22, 0.18) if shards else 1.0
    values = jax.random.normal(key, extent, jnp.float32) * scale * loudness
    return jnp.minimum(jnp.maximum(values, -limit), limit).astype(kind)


def setup_inputs(seed: int = 0) -> dict:
    key_of = jax.random.split(jax.random.key(seed), 7)
    query = draw_query(jax.random.fold_in(key_of[6], 71), 0)
    key = draw_key(jax.random.fold_in(key_of[6], 71), 0)
    value = scatter_about(key_of[2], (DOC_TOK, HEADS * HEAD_DIM), 1.0, 6.0, ((0, 16), (1, 2)))
    d_out = scatter_about(key_of[3], (CAD_TOK, HEADS * HEAD_DIM), 1.0, 6.0, ((0, 32),))
    seg_map = jnp.searchsorted(jnp.cumsum(uneven(key_of[4], SEGS, CAD_BLOCKS, 8, 2)), jnp.arange(CAD_BLOCKS), side="right").astype(jnp.int32)
    spans = picks_of(key_of[5], SEGS, DOC_BLOCKS, SPANS, 8192)
    return {"query": query, "key": key, "value": value, "d_out": d_out, "seg_map": seg_map, "spans": spans}


def reference(query, key, value, d_out, seg_map, spans):
    factor = 1.0 / math.sqrt(HEAD_DIM)
    group_blocks = ROWS_GROUP // BLOCK
    all_width = HEADS * HEAD_DIM
    block_ids = spans[seg_map].astype(jnp.int32)
    key_blocks = key.reshape(DOC_BLOCKS, BLOCK, HEADS, HEAD_DIM)
    value_blocks = value.reshape(DOC_BLOCKS, BLOCK, HEADS, HEAD_DIM)

    def one_group(carry, inputs):
        query_group, dout_group, group_ids = inputs
        query_four = query_group.reshape(group_blocks, BLOCK, HEADS, HEAD_DIM).astype(jnp.float32)
        dout_four = dout_group.reshape(group_blocks, BLOCK, HEADS, HEAD_DIM).astype(jnp.float32)
        key_tiles = key_blocks[group_ids].reshape(group_blocks, SPANS * BLOCK, HEADS, HEAD_DIM).astype(jnp.float32)
        value_tiles = value_blocks[group_ids].reshape(group_blocks, SPANS * BLOCK, HEADS, HEAD_DIM).astype(jnp.float32)
        scores = jnp.einsum('cqhd,ckhd->chqk', query_four, key_tiles) * factor
        top_score = lax.optimization_barrier(jnp.max(scores, axis=-1, keepdims=True))
        expo = jnp.exp(scores - top_score)
        prob = expo / lax.optimization_barrier(jnp.sum(expo, axis=-1, keepdims=True))
        prob_b = prob.astype(jnp.bfloat16).astype(jnp.float32)
        attn = jnp.einsum('chqk,ckhd->cqhd', prob_b, value_tiles)
        delta = lax.optimization_barrier(jnp.sum(dout_four * attn, axis=-1))
        delta = jnp.transpose(delta, (0, 2, 1))[..., None]
        dprob = jnp.einsum('cqhd,ckhd->chqk', dout_four, value_tiles)
        dscore_b = (prob * (dprob - delta)).astype(jnp.bfloat16).astype(jnp.float32)
        grad_query = (jnp.einsum('chqk,ckhd->cqhd', dscore_b, key_tiles) * factor).astype(jnp.bfloat16)
        key_slots = jnp.einsum('chqk,cqhd->ckhd', dscore_b, query_four) * factor
        value_slots = jnp.einsum('chqk,cqhd->ckhd', prob_b, dout_four)
        flat_ids = group_ids.reshape(group_blocks * SPANS)
        key_sum = carry[0].at[flat_ids].add(key_slots.reshape(group_blocks * SPANS, BLOCK, all_width))
        value_sum = carry[1].at[flat_ids].add(value_slots.reshape(group_blocks * SPANS, BLOCK, all_width))
        outputs = (attn.astype(jnp.bfloat16).reshape(ROWS_GROUP, all_width), grad_query.reshape(ROWS_GROUP, all_width))
        return ((key_sum, value_sum), outputs)
    start_sums = (jnp.zeros((DOC_BLOCKS, BLOCK, all_width), jnp.float32), jnp.zeros((DOC_BLOCKS, BLOCK, all_width), jnp.float32))
    inputs = (query.reshape(N_BLK, ROWS_GROUP, all_width), d_out.reshape(N_BLK, ROWS_GROUP, all_width), block_ids.reshape(N_BLK, group_blocks, SPANS))
    (key_sum, value_sum), (attn_all, grad_all) = lax.scan(one_group, start_sums, inputs)
    attn_out = attn_all.reshape(CAD_TOK, all_width)
    d_query = grad_all.reshape(CAD_TOK, all_width)
    d_key = key_sum.reshape(DOC_TOK, all_width).astype(jnp.bfloat16)
    d_value = value_sum.reshape(DOC_TOK, all_width).astype(jnp.bfloat16)
    return (attn_out, d_query, d_key, d_value)
```

```python
import functools
import math

import jax, jax.numpy as jnp
from jax import lax
from jax.experimental import pallas as pl
from jax.experimental.pallas import tpu as pltpu
from jax.sharding import PartitionSpec as P


HEADS = 32
HEAD_DIM = 128
BLOCK = 128
SPANS = 8
NT = (((1,), (1,)), ((), ()))


def attend_block(q, do, k_cat, v_cat, kt_cat, vt_cat, factor):
    f32 = jnp.float32
    s = lax.dot_general(k_cat, q, NT, preferred_element_type=f32)
    dp = lax.dot_general(v_cat, do, NT, preferred_element_type=f32)
    top = jnp.max(s, axis=0, keepdims=True)
    e = jnp.exp((s - top) * factor)
    inv = 1.0 / jnp.sum(e, axis=0, keepdims=True)
    p = e * inv
    delta = jnp.sum(p * dp, axis=0, keepdims=True)
    pb = p.astype(jnp.bfloat16)
    ds = (p * (dp - delta)).astype(jnp.bfloat16)
    attn_t = jnp.dot(vt_cat, pb, preferred_element_type=f32)
    dq_t = jnp.dot(kt_cat, ds, preferred_element_type=f32) * factor
    dv = jnp.dot(pb, do, preferred_element_type=f32)
    dk = jnp.dot(ds, q, preferred_element_type=f32)
    return attn_t.T.astype(jnp.bfloat16), dq_t.T.astype(jnp.bfloat16), dk, dv


def attend_kernel(unroll, spans_n, factor, ids_ref, q_ref, do_ref, k_ref, v_ref, at_ref, dq_ref, dk_ref, dv_ref, kt, vt, dka, dva):
    step = pl.program_id(0)
    docs = k_ref.shape[0]

    @pl.when(step == 0)
    def _():
        dka[...] = jnp.zeros_like(dka)
        dva[...] = jnp.zeros_like(dva)
        for d in range(docs):
            kt[d] = k_ref[d].T
            vt[d] = v_ref[d].T

    outs = []
    for u in range(unroll):
        ids = [ids_ref[step * unroll + u, j] for j in range(spans_n)]
        q, do = q_ref[u], do_ref[u]
        k_cat = jnp.concatenate([k_ref[i] for i in ids], axis=0)
        v_cat = jnp.concatenate([v_ref[i] for i in ids], axis=0)
        kt_cat = jnp.concatenate([kt[i] for i in ids], axis=1)
        vt_cat = jnp.concatenate([vt[i] for i in ids], axis=1)
        outs.append((ids, attend_block(q, do, k_cat, v_cat, kt_cat, vt_cat, factor)))
    for u, (ids, (at, dq, dk, dv)) in enumerate(outs):
        at_ref[u] = at
        dq_ref[u] = dq
        for j, i in enumerate(ids):
            dka[i] += dk[j * 128:(j + 1) * 128]
            dva[i] += dv[j * 128:(j + 1) * 128]

    @pl.when(step == pl.num_programs(0) - 1)
    def _():
        dk_ref[...] = (dka[...] * factor).astype(jnp.bfloat16)
        dv_ref[...] = dva[...].astype(jnp.bfloat16)


def attend(ids, q, do, k, v, unroll=2):
    blocks, rows, width = q.shape
    docs = k.shape[0]
    factor = 1.0 / math.sqrt(width)
    per = pl.BlockSpec((unroll, rows, width), lambda c, ids: (c, 0, 0))
    whole = pl.BlockSpec((docs, rows, width), lambda c, ids: (0, 0, 0))
    return pl.pallas_call(
        functools.partial(attend_kernel, unroll, ids.shape[1], factor),
        out_shape=[jax.ShapeDtypeStruct(q.shape, q.dtype)] * 2 + [jax.ShapeDtypeStruct(k.shape, k.dtype)] * 2,
        grid_spec=pltpu.PrefetchScalarGridSpec(
            num_scalar_prefetch=1, grid=(blocks // unroll,),
            in_specs=[per, per, whole, whole], out_specs=[per, per, whole, whole],
            scratch_shapes=[pltpu.VMEM(k.shape, k.dtype)] * 2 + [pltpu.VMEM(k.shape, jnp.float32)] * 2),
        compiler_params=pltpu.CompilerParams(dimension_semantics=("arbitrary",), vmem_limit_bytes=60 << 20),
        name="attend",
    )(ids, q, do, k, v)

def head_pass(q_head, dout_head, key_head, value_head, id_groups):
    factor = 1.0 / math.sqrt(HEAD_DIM)
    group_width = q_head.shape[1]
    doc_blocks = key_head.shape[0]

    def one_group(sums, inputs):
        q_group, dout_group, group_ids = inputs
        flat_ids = group_ids.reshape(group_width * SPANS)
        key_tiles = jnp.take(key_head, flat_ids, axis=0).reshape(
            group_width, SPANS * BLOCK, HEAD_DIM
        )
        value_tiles = jnp.take(value_head, flat_ids, axis=0).reshape(
            group_width, SPANS * BLOCK, HEAD_DIM
        )
        scores = (
            jnp.einsum("cqd,ckd->cqk", q_group, key_tiles, preferred_element_type=jnp.float32)
            * factor
        )
        top_score = jnp.max(scores, axis=-1, keepdims=True)
        expo = jnp.exp(scores - top_score)
        prob = expo / jnp.sum(expo, axis=-1, keepdims=True)
        prob_b = prob.astype(jnp.bfloat16)
        attn = jnp.einsum("cqk,ckd->cqd", prob_b, value_tiles, preferred_element_type=jnp.float32)
        delta = jnp.sum(dout_group.astype(jnp.float32) * attn, axis=-1, keepdims=True)
        dprob = jnp.einsum(
            "cqd,ckd->cqk", dout_group, value_tiles, preferred_element_type=jnp.float32
        )
        dscore_b = (prob * (dprob - delta)).astype(jnp.bfloat16)
        grad_query = (
            jnp.einsum("cqk,ckd->cqd", dscore_b, key_tiles, preferred_element_type=jnp.float32)
            * factor
        ).astype(jnp.bfloat16)
        key_slots = (
            jnp.einsum("cqk,cqd->ckd", dscore_b, q_group, preferred_element_type=jnp.float32)
            * factor
        )
        value_slots = jnp.einsum(
            "cqk,cqd->ckd", prob_b, dout_group, preferred_element_type=jnp.float32
        )
        one_hot = (jnp.arange(doc_blocks, dtype=jnp.int32)[:, None] == flat_ids[None, :]).astype(
            jnp.float32
        )
        key_sums = sums[0] + jnp.dot(
            one_hot,
            key_slots.reshape(group_width * SPANS, BLOCK * HEAD_DIM),
            precision=lax.Precision.HIGHEST,
            preferred_element_type=jnp.float32,
        )
        value_sums = sums[1] + jnp.dot(
            one_hot,
            value_slots.reshape(group_width * SPANS, BLOCK * HEAD_DIM),
            precision=lax.Precision.HIGHEST,
            preferred_element_type=jnp.float32,
        )
        return ((key_sums, value_sums), (attn.astype(jnp.bfloat16), grad_query))

    zero_sums = jnp.zeros((doc_blocks, BLOCK * HEAD_DIM), jnp.float32)
    (key_sums, value_sums), (attn_head, grad_head) = lax.scan(
        one_group, (zero_sums, zero_sums), (q_head, dout_head, id_groups)
    )
    return (attn_head, grad_head, key_sums, value_sums)


def block_table(global_blocks, seg_map, spans):
    block_count = global_blocks.shape[0]
    seg_match = (
        global_blocks[:, None] == jnp.arange(seg_map.shape[0], dtype=jnp.int32)[None, :]
    ).astype(jnp.int32)
    seg_here = jnp.sum(seg_match * seg_map[None, :], axis=1)
    span_match = (seg_here[:, None] == jnp.arange(spans.shape[0], dtype=jnp.int32)[None, :]).astype(
        jnp.int32
    )
    block_ids = jnp.sum(span_match[:, :, None] * spans[None, :, :], axis=1)
    group_width = math.gcd(block_count, max(1, 512 // BLOCK))
    group_count = block_count // group_width
    return (block_ids.reshape(group_count, group_width, SPANS), group_count, group_width)


def by_heads(array, heads_count, group_count, group_width):
    block_count = group_count * group_width
    shaped = array.reshape(block_count, BLOCK, heads_count, HEAD_DIM).transpose(2, 0, 1, 3)
    return shaped.reshape(heads_count, group_count, group_width, BLOCK, HEAD_DIM)


def from_heads(array, heads_count):
    row_count = array.shape[1] * array.shape[2] * BLOCK
    shaped = array.reshape(heads_count, row_count, HEAD_DIM).transpose(1, 0, 2)
    return shaped.reshape(row_count, heads_count * HEAD_DIM)


def from_head_sums(array, heads_count):
    doc_rows = array.shape[1] // HEAD_DIM * BLOCK // BLOCK * array.shape[0] // array.shape[0]
    doc_rows = array.shape[1] * array.shape[2] // (BLOCK * HEAD_DIM) * BLOCK
    shaped = array.reshape(heads_count, doc_rows, HEAD_DIM).transpose(1, 0, 2)
    return shaped.reshape(doc_rows, heads_count * HEAD_DIM)


def body_shared(query, key, value, d_out, seg_map, spans):
    dummy_carry = jnp.zeros((), jnp.int32)
    heads_here = HEADS // lax.axis_size("blk")
    q_rows, dout_rows = (
        lax.all_to_all(query, "blk", split_axis=1, concat_axis=0, tiled=True),
        lax.all_to_all(d_out, "blk", split_axis=1, concat_axis=0, tiled=True),
    )
    per_device = query.shape[0] // BLOCK
    block_count = q_rows.shape[0] // BLOCK
    local_blocks = jnp.arange(block_count, dtype=jnp.int32)
    global_blocks = (
        local_blocks // per_device * lax.axis_size("head") + lax.axis_index("head")
    ) * per_device + local_blocks % per_device
    id_groups, group_count, group_width = block_table(global_blocks, seg_map, spans)
    q_heads = by_heads(q_rows, heads_here, group_count, group_width)
    dout_heads = by_heads(dout_rows, heads_here, group_count, group_width)
    key_wide, value_wide = (
        lax.all_gather(key, "head", axis=1, tiled=True),
        lax.all_gather(value, "head", axis=1, tiled=True),
    )
    key_cols, value_cols = (
        lax.all_to_all(key_wide, "blk", split_axis=1, concat_axis=0, tiled=True),
        lax.all_to_all(value_wide, "blk", split_axis=1, concat_axis=0, tiled=True),
    )
    doc_blocks = key_cols.shape[0] // BLOCK

    def to_blocks(array):
        return array.reshape(doc_blocks, BLOCK, heads_here, HEAD_DIM).transpose(2, 0, 1, 3)

    def scan_head(carry, inputs):
        q_head, dout_head, key_head, value_head = inputs
        return (carry, head_pass(q_head, dout_head, key_head, value_head, id_groups))

    _, (attn_heads, grad_heads, key_parts, value_parts) = lax.scan(
        scan_head, dummy_carry, (q_heads, dout_heads, to_blocks(key_cols), to_blocks(value_cols))
    )
    key_back, value_back = (
        lax.all_to_all(
            from_head_sums(key_parts, heads_here).astype(jnp.bfloat16),
            "blk",
            split_axis=0,
            concat_axis=1,
            tiled=True,
        ).astype(jnp.float32),
        lax.all_to_all(
            from_head_sums(value_parts, heads_here).astype(jnp.bfloat16),
            "blk",
            split_axis=0,
            concat_axis=1,
            tiled=True,
        ).astype(jnp.float32),
    )
    key_total, value_total = (
        lax.psum_scatter(
            key_back.astype(jnp.bfloat16), "head", scatter_dimension=1, tiled=True
        ).astype(jnp.float32),
        lax.psum_scatter(
            value_back.astype(jnp.bfloat16), "head", scatter_dimension=1, tiled=True
        ).astype(jnp.float32),
    )
    attn_out, d_query = (
        lax.all_to_all(
            from_heads(attn_heads, heads_here), "blk", split_axis=0, concat_axis=1, tiled=True
        ),
        lax.all_to_all(
            from_heads(grad_heads, heads_here), "blk", split_axis=0, concat_axis=1, tiled=True
        ),
    )
    return (attn_out, d_query, key_total.astype(jnp.bfloat16), value_total.astype(jnp.bfloat16))


def body(query, key, value, d_out, seg_map, spans):
    both = ("blk", "head")
    blks, columns = lax.axis_size("blk"), lax.axis_size("head")
    ids = spans[seg_map].astype(jnp.int32)

    def cad_out(array):
        split = array.reshape(array.shape[0], columns, blks, HEAD_DIM).transpose(2, 1, 0, 3)
        split = split.reshape(blks * columns, array.shape[0], HEAD_DIM)
        return lax.all_to_all(split, both, split_axis=0, concat_axis=0, tiled=True)

    def cad_back(array):
        back = lax.all_to_all(array, both, split_axis=0, concat_axis=0, tiled=True)
        back = back.reshape(blks, columns, array.shape[1], HEAD_DIM).transpose(2, 1, 0, 3)
        return back.reshape(array.shape[1], HEADS * HEAD_DIM)

    def doc_out(array):
        split = array.reshape(array.shape[0], blks, HEAD_DIM).transpose(1, 0, 2)
        return lax.all_to_all(split, "blk", split_axis=0, concat_axis=0, tiled=True)

    def doc_back(array):
        back = lax.all_to_all(array, "blk", split_axis=0, concat_axis=0, tiled=True)
        return back.transpose(1, 0, 2).reshape(array.shape[1], blks * HEAD_DIM)

    q, do, k, v = cad_out(query), cad_out(d_out), doc_out(key), doc_out(value)
    at, dq, dk, dv = attend(ids, q, do, k, v)
    return cad_back(at), cad_back(dq), doc_back(dk), doc_back(dv)


def one_head_each(mesh):
    return mesh.shape["blk"] * mesh.shape["head"] == HEADS


def solution(mesh):
    placed = (
        P(("blk", "head"), None),
        P("blk", "head"),
        P("blk", "head"),
        P(("blk", "head"), None),
        P(),
        P(),
    )
    return jax.shard_map(
        body if one_head_each(mesh) else body_shared,
        mesh=mesh,
        in_specs=placed,
        out_specs=(
            P(("blk", "head"), None),
            P(("blk", "head"), None),
            P("blk", "head"),
            P("blk", "head"),
        ),
        check_vma=False,
    )
```

```python
import functools
import math

import jax
import jax.numpy as jnp
from jax import lax
from jax.experimental import pallas as pl
from jax.experimental.pallas import tpu as pltpu
from jax.sharding import PartitionSpec as P

HEADS = 32
HEAD_DIM = 128
BLOCK = 128
SPANS = 8

NT = (((1,), (1,)), ((), ()))
MESH = pl.DeviceIdType.MESH


def attend_block(q, do, k_cat, v_cat, kt_cat, vt_cat, factor):
    f32 = jnp.float32
    s = lax.dot_general(k_cat, q, NT, preferred_element_type=f32)
    dp = lax.dot_general(v_cat, do, NT, preferred_element_type=f32)
    top = jnp.max(s, axis=0, keepdims=True)
    e = jnp.exp((s - top) * factor)
    inv = 1.0 / jnp.sum(e, axis=0, keepdims=True)
    p = e * inv
    delta = jnp.sum(p * dp, axis=0, keepdims=True)
    pb = p.astype(jnp.bfloat16)
    ds = (p * (dp - delta)).astype(jnp.bfloat16)
    attn_t = jnp.dot(vt_cat, pb, preferred_element_type=f32)
    dq_t = jnp.dot(kt_cat, ds, preferred_element_type=f32) * factor
    return attn_t.T.astype(jnp.bfloat16), dq_t.T.astype(jnp.bfloat16), pb, ds


def fused_kernel(
    blks, columns, unroll, factor,
    ids_ref, slot_ref, q_in, do_in, k_in, v_in,
    at_out, dq_out, dk_out, dv_out,
    q_s, do_s, k_s, v_s, kt, vt, p_s, ds_s, at_s, dq_s, dk_s, dv_s,
    in_send, out_send, kv_recv, q_recv, do_recv, out_recv,
):
    count = blks * columns
    docs = k_s.shape[0]
    per_blk = docs // blks
    blk, col = lax.axis_index("blk"), lax.axis_index("head")
    me = blk * columns + col
    my_head = col * blks + blk

    def cols(index):
        return pl.ds(pl.multiple_of(index * HEAD_DIM, HEAD_DIM), HEAD_DIM)

    def place(t):
        to = lax.rem(me + t, count)
        return to // columns, lax.rem(to, columns)

    def remote(src, dst, send, recv, where):
        pltpu.make_async_remote_copy(
            src_ref=src, dst_ref=dst, send_sem=send, recv_sem=recv,
            device_id=where, device_id_type=MESH,
        ).start()

    barrier = pltpu.get_barrier_semaphore()

    @pl.loop(1, count)
    def _(t):
        pl.semaphore_signal(barrier, inc=1, device_id=place(t), device_id_type=MESH)

    pltpu.make_async_copy(k_in.at[:, cols(blk)], k_s.at[blk], kv_recv.at[0]).start()
    pltpu.make_async_copy(v_in.at[:, cols(blk)], v_s.at[blk], kv_recv.at[1]).start()
    pltpu.make_async_copy(q_in.at[:, cols(my_head)], q_s.at[me], q_recv.at[me]).start()
    pltpu.make_async_copy(do_in.at[:, cols(my_head)], do_s.at[me], do_recv.at[me]).start()
    pl.semaphore_wait(barrier, count - 1)

    @pl.loop(1, blks)
    def _(t):
        to = lax.rem(blk + t, blks)
        remote(k_in.at[:, cols(to)], k_s.at[blk], in_send.at[0], kv_recv.at[0], (to, col))
        remote(v_in.at[:, cols(to)], v_s.at[blk], in_send.at[1], kv_recv.at[1], (to, col))

    @pl.loop(1, count)
    def _(t):
        b, c = place(t)
        head = c * blks + b
        remote(q_in.at[:, cols(head)], q_s.at[me], in_send.at[2], q_recv.at[me], (b, c))
        remote(do_in.at[:, cols(head)], do_s.at[me], in_send.at[3], do_recv.at[me], (b, c))

    @pl.loop(0, count)
    def _(c):
        p_s[c, SPANS] = jnp.zeros((BLOCK, BLOCK), jnp.bfloat16)
        ds_s[c, SPANS] = jnp.zeros((BLOCK, BLOCK), jnp.bfloat16)

    pltpu.make_async_copy(k_s, k_s, kv_recv.at[0]).wait()
    pltpu.make_async_copy(v_s, v_s, kv_recv.at[1]).wait()
    @pl.loop(0, docs)
    def _(d):
        kt[d] = k_s[d].T
        vt[d] = v_s[d].T

    def source(t):
        return lax.rem(me + count - t, count)

    def send_rows(t):
        c = source(t)
        where = (c // columns, lax.rem(c, columns))
        here = cols(my_head)

        @pl.when(t == 0)
        def _():
            pltpu.make_async_copy(at_s.at[c], at_out.at[:, here], out_recv.at[0]).start()
            pltpu.make_async_copy(dq_s.at[c], dq_out.at[:, here], out_recv.at[1]).start()

        @pl.when(t > 0)
        def _():
            remote(at_s.at[c], at_out.at[:, here], out_send.at[0], out_recv.at[0], where)
            remote(dq_s.at[c], dq_out.at[:, here], out_send.at[1], out_recv.at[1], where)

    @pl.loop(0, count // unroll)
    def _(step):
        @pl.when(step > 0)
        def _():
            for u in range(unroll):
                send_rows((step - 1) * unroll + u)

        for u in range(unroll):
            c = source(step * unroll + u)
            pltpu.make_async_copy(q_s.at[c], q_s.at[c], q_recv.at[c]).wait()
            pltpu.make_async_copy(do_s.at[c], do_s.at[c], do_recv.at[c]).wait()
        results = []
        for u in range(unroll):
            c = source(step * unroll + u)
            ids = [ids_ref[c, j] for j in range(SPANS)]
            k_cat = jnp.concatenate([k_s[i] for i in ids], axis=0)
            v_cat = jnp.concatenate([v_s[i] for i in ids], axis=0)
            kt_cat = jnp.concatenate([kt[i] for i in ids], axis=1)
            vt_cat = jnp.concatenate([vt[i] for i in ids], axis=1)
            results.append((c, attend_block(q_s[c], do_s[c], k_cat, v_cat, kt_cat, vt_cat, factor)))
        for c, (at, dq, pb, ds) in results:
            at_s[c] = at
            dq_s[c] = dq
            p_s[c, 0:SPANS] = pb.reshape(SPANS, BLOCK, BLOCK)
            ds_s[c, 0:SPANS] = ds.reshape(SPANS, BLOCK, BLOCK)

    for u in range(unroll):
        send_rows(count - unroll + u)

    def send_doc(t):
        to = lax.rem(blk + t, blks)

        @pl.when(t == 0)
        def _():
            pltpu.make_async_copy(dk_s.at[to], dk_out.at[:, cols(blk)], out_recv.at[2]).start()
            pltpu.make_async_copy(dv_s.at[to], dv_out.at[:, cols(blk)], out_recv.at[3]).start()

        @pl.when(t > 0)
        def _():
            remote(dk_s.at[to], dk_out.at[:, cols(blk)], out_send.at[2], out_recv.at[2], (to, col))
            remote(dv_s.at[to], dv_out.at[:, cols(blk)], out_send.at[3], out_recv.at[3], (to, col))

    pair, chunk = 2, 8

    @pl.loop(0, docs // pair)
    def _(step):
        @pl.when(step > 0)
        def _():
            for u in range(pair):
                send_doc((step - 1) * pair + u)

        to = [lax.rem(blk + step * pair + u, blks) for u in range(pair)]
        for held, right, out, scale in ((ds_s, q_s, dk_s, factor), (p_s, do_s, dv_s, None)):
            def part(i, total):
                left = jnp.concatenate([
                    jnp.concatenate([held[i * chunk + c, slot_ref[i * chunk + c, d]] for c in range(chunk)], axis=1)
                    for d in to], axis=0)
                rows = right[pl.ds(i * chunk, chunk)].reshape(chunk * BLOCK, HEAD_DIM)
                return total + jnp.dot(left, rows, preferred_element_type=jnp.float32)
            total = lax.fori_loop(0, count // chunk, part, jnp.zeros((pair * BLOCK, HEAD_DIM), jnp.float32))
            if scale is not None:
                total = total * scale
            for u, d in enumerate(to):
                out[d] = total[u * BLOCK:(u + 1) * BLOCK].astype(jnp.bfloat16)

    for u in range(pair):
        send_doc(docs - pair + u)

    def drain(array, blocks, sem):
        view = array.at[pl.ds(0, blocks)]
        pltpu.make_async_copy(view, view, sem).wait()

    drain(k_s, blks - 1, in_send.at[0])
    drain(v_s, blks - 1, in_send.at[1])
    drain(q_s, count - 1, in_send.at[2])
    drain(do_s, count - 1, in_send.at[3])
    drain(at_s, count - 1, out_send.at[0])
    drain(dq_s, count - 1, out_send.at[1])
    drain(dk_s, blks - 1, out_send.at[2])
    drain(dv_s, blks - 1, out_send.at[3])
    drain(at_s, count, out_recv.at[0])
    drain(dq_s, count, out_recv.at[1])
    drain(dk_s, docs, out_recv.at[2])
    drain(dv_s, docs, out_recv.at[3])


def body(query, key, value, d_out, seg_map, spans):
    blks, columns = lax.axis_size("blk"), lax.axis_size("head")
    count = blks * columns
    docs = key.shape[0] // BLOCK * blks
    ids = spans[seg_map].astype(jnp.int32)
    match = ids[:, :, None] == jnp.arange(docs, dtype=jnp.int32)
    place = jnp.arange(SPANS, dtype=jnp.int32)[None, :, None]
    slot = jnp.min(jnp.where(match, place, SPANS), axis=1)
    bf16 = jnp.bfloat16
    rows, tiles = (count, BLOCK, HEAD_DIM), (docs, BLOCK, HEAD_DIM)
    anywhere = pl.BlockSpec(memory_space=pl.ANY)
    scalars = pl.BlockSpec(memory_space=pltpu.SMEM)
    return pl.pallas_call(
        functools.partial(fused_kernel, blks, columns, 2, 1.0 / math.sqrt(HEAD_DIM)),
        out_shape=[jax.ShapeDtypeStruct(a.shape, a.dtype) for a in (query, query, key, value)],
        in_specs=[scalars] * 2 + [anywhere] * 4,
        out_specs=[anywhere] * 4,
        scratch_shapes=[
            pltpu.VMEM(rows, bf16), pltpu.VMEM(rows, bf16),
            pltpu.VMEM(tiles, bf16), pltpu.VMEM(tiles, bf16),
            pltpu.VMEM(tiles, bf16), pltpu.VMEM(tiles, bf16),
            pltpu.VMEM((count, SPANS + 1, BLOCK, BLOCK), bf16),
            pltpu.VMEM((count, SPANS + 1, BLOCK, BLOCK), bf16),
            pltpu.VMEM(rows, bf16), pltpu.VMEM(rows, bf16),
            pltpu.VMEM(tiles, bf16), pltpu.VMEM(tiles, bf16),
            pltpu.SemaphoreType.DMA((4,)), pltpu.SemaphoreType.DMA((4,)),
            pltpu.SemaphoreType.DMA((2,)), pltpu.SemaphoreType.DMA((count,)),
            pltpu.SemaphoreType.DMA((count,)), pltpu.SemaphoreType.DMA((4,)),
        ],
        compiler_params=pltpu.CompilerParams(
            collective_id=0, has_side_effects=True, vmem_limit_bytes=60 << 20
        ),
        name="attend",
    )(ids, slot, query, d_out, key, value)


def fits_one_head_each(mesh):
    return mesh.shape["blk"] * mesh.shape["head"] == HEADS


def head_pass(q_head, dout_head, key_head, value_head, id_groups):
    factor = 1.0 / math.sqrt(HEAD_DIM)
    group_width = q_head.shape[1]
    doc_blocks = key_head.shape[0]

    def one_group(sums, inputs):
        q_group, dout_group, group_ids = inputs
        flat_ids = group_ids.reshape(group_width * SPANS)
        key_tiles = jnp.take(key_head, flat_ids, axis=0).reshape(
            group_width, SPANS * BLOCK, HEAD_DIM
        )
        value_tiles = jnp.take(value_head, flat_ids, axis=0).reshape(
            group_width, SPANS * BLOCK, HEAD_DIM
        )
        scores = (
            jnp.einsum("cqd,ckd->cqk", q_group, key_tiles, preferred_element_type=jnp.float32)
            * factor
        )
        top_score = jnp.max(scores, axis=-1, keepdims=True)
        expo = jnp.exp(scores - top_score)
        prob = expo / jnp.sum(expo, axis=-1, keepdims=True)
        prob_b = prob.astype(jnp.bfloat16)
        attn = jnp.einsum("cqk,ckd->cqd", prob_b, value_tiles, preferred_element_type=jnp.float32)
        delta = jnp.sum(dout_group.astype(jnp.float32) * attn, axis=-1, keepdims=True)
        dprob = jnp.einsum(
            "cqd,ckd->cqk", dout_group, value_tiles, preferred_element_type=jnp.float32
        )
        dscore_b = (prob * (dprob - delta)).astype(jnp.bfloat16)
        grad_query = (
            jnp.einsum("cqk,ckd->cqd", dscore_b, key_tiles, preferred_element_type=jnp.float32)
            * factor
        ).astype(jnp.bfloat16)
        key_slots = (
            jnp.einsum("cqk,cqd->ckd", dscore_b, q_group, preferred_element_type=jnp.float32)
            * factor
        )
        value_slots = jnp.einsum(
            "cqk,cqd->ckd", prob_b, dout_group, preferred_element_type=jnp.float32
        )
        one_hot = (jnp.arange(doc_blocks, dtype=jnp.int32)[:, None] == flat_ids[None, :]).astype(
            jnp.float32
        )
        key_sums = sums[0] + jnp.dot(
            one_hot,
            key_slots.reshape(group_width * SPANS, BLOCK * HEAD_DIM),
            precision=lax.Precision.HIGHEST,
            preferred_element_type=jnp.float32,
        )
        value_sums = sums[1] + jnp.dot(
            one_hot,
            value_slots.reshape(group_width * SPANS, BLOCK * HEAD_DIM),
            precision=lax.Precision.HIGHEST,
            preferred_element_type=jnp.float32,
        )
        return ((key_sums, value_sums), (attn.astype(jnp.bfloat16), grad_query))

    zero_sums = jnp.zeros((doc_blocks, BLOCK * HEAD_DIM), jnp.float32)
    (key_sums, value_sums), (attn_head, grad_head) = lax.scan(
        one_group, (zero_sums, zero_sums), (q_head, dout_head, id_groups)
    )
    return (attn_head, grad_head, key_sums, value_sums)


def block_table(global_blocks, seg_map, spans):
    block_count = global_blocks.shape[0]
    seg_match = (
        global_blocks[:, None] == jnp.arange(seg_map.shape[0], dtype=jnp.int32)[None, :]
    ).astype(jnp.int32)
    seg_here = jnp.sum(seg_match * seg_map[None, :], axis=1)
    span_match = (seg_here[:, None] == jnp.arange(spans.shape[0], dtype=jnp.int32)[None, :]).astype(
        jnp.int32
    )
    block_ids = jnp.sum(span_match[:, :, None] * spans[None, :, :], axis=1)
    group_width = math.gcd(block_count, max(1, 512 // BLOCK))
    group_count = block_count // group_width
    return (block_ids.reshape(group_count, group_width, SPANS), group_count, group_width)


def by_heads(array, heads_count, group_count, group_width):
    block_count = group_count * group_width
    shaped = array.reshape(block_count, BLOCK, heads_count, HEAD_DIM).transpose(2, 0, 1, 3)
    return shaped.reshape(heads_count, group_count, group_width, BLOCK, HEAD_DIM)


def from_heads(array, heads_count):
    row_count = array.shape[1] * array.shape[2] * BLOCK
    shaped = array.reshape(heads_count, row_count, HEAD_DIM).transpose(1, 0, 2)
    return shaped.reshape(row_count, heads_count * HEAD_DIM)


def from_head_sums(array, heads_count):
    doc_rows = array.shape[1] // HEAD_DIM * BLOCK // BLOCK * array.shape[0] // array.shape[0]
    doc_rows = array.shape[1] * array.shape[2] // (BLOCK * HEAD_DIM) * BLOCK
    shaped = array.reshape(heads_count, doc_rows, HEAD_DIM).transpose(1, 0, 2)
    return shaped.reshape(doc_rows, heads_count * HEAD_DIM)


def body_shared(query, key, value, d_out, seg_map, spans):
    dummy_carry = jnp.zeros((), jnp.int32)
    heads_here = HEADS // lax.axis_size("blk")
    q_rows, dout_rows = (
        lax.all_to_all(query, "blk", split_axis=1, concat_axis=0, tiled=True),
        lax.all_to_all(d_out, "blk", split_axis=1, concat_axis=0, tiled=True),
    )
    per_device = query.shape[0] // BLOCK
    block_count = q_rows.shape[0] // BLOCK
    local_blocks = jnp.arange(block_count, dtype=jnp.int32)
    global_blocks = (
        local_blocks // per_device * lax.axis_size("head") + lax.axis_index("head")
    ) * per_device + local_blocks % per_device
    id_groups, group_count, group_width = block_table(global_blocks, seg_map, spans)
    q_heads = by_heads(q_rows, heads_here, group_count, group_width)
    dout_heads = by_heads(dout_rows, heads_here, group_count, group_width)
    key_wide, value_wide = (
        lax.all_gather(key, "head", axis=1, tiled=True),
        lax.all_gather(value, "head", axis=1, tiled=True),
    )
    key_cols, value_cols = (
        lax.all_to_all(key_wide, "blk", split_axis=1, concat_axis=0, tiled=True),
        lax.all_to_all(value_wide, "blk", split_axis=1, concat_axis=0, tiled=True),
    )
    doc_blocks = key_cols.shape[0] // BLOCK

    def to_blocks(array):
        return array.reshape(doc_blocks, BLOCK, heads_here, HEAD_DIM).transpose(2, 0, 1, 3)

    def scan_head(carry, inputs):
        q_head, dout_head, key_head, value_head = inputs
        return (carry, head_pass(q_head, dout_head, key_head, value_head, id_groups))

    _, (attn_heads, grad_heads, key_parts, value_parts) = lax.scan(
        scan_head, dummy_carry, (q_heads, dout_heads, to_blocks(key_cols), to_blocks(value_cols))
    )
    key_back, value_back = (
        lax.all_to_all(
            from_head_sums(key_parts, heads_here).astype(jnp.bfloat16),
            "blk",
            split_axis=0,
            concat_axis=1,
            tiled=True,
        ).astype(jnp.float32),
        lax.all_to_all(
            from_head_sums(value_parts, heads_here).astype(jnp.bfloat16),
            "blk",
            split_axis=0,
            concat_axis=1,
            tiled=True,
        ).astype(jnp.float32),
    )
    key_total, value_total = (
        lax.psum_scatter(
            key_back.astype(jnp.bfloat16), "head", scatter_dimension=1, tiled=True
        ).astype(jnp.float32),
        lax.psum_scatter(
            value_back.astype(jnp.bfloat16), "head", scatter_dimension=1, tiled=True
        ).astype(jnp.float32),
    )
    attn_out, d_query = (
        lax.all_to_all(
            from_heads(attn_heads, heads_here), "blk", split_axis=0, concat_axis=1, tiled=True
        ),
        lax.all_to_all(
            from_heads(grad_heads, heads_here), "blk", split_axis=0, concat_axis=1, tiled=True
        ),
    )
    return (attn_out, d_query, key_total.astype(jnp.bfloat16), value_total.astype(jnp.bfloat16))


def solution(mesh):
    placed = (
        P(("blk", "head"), None),
        P("blk", "head"),
        P("blk", "head"),
        P(("blk", "head"), None),
        P(),
        P(),
    )
    return jax.shard_map(
        body if fits_one_head_each(mesh) else body_shared,
        mesh=mesh,
        in_specs=placed,
        out_specs=(
            P(("blk", "head"), None),
            P(("blk", "head"), None),
            P("blk", "head"),
            P("blk", "head"),
        ),
        check_vma=False,
    )
```

```python
import functools
import math

import jax
import jax.numpy as jnp
from jax import lax
from jax.experimental import pallas as pl
from jax.experimental.pallas import tpu as pltpu
from jax.sharding import PartitionSpec as P

HEADS = 32
HEAD_DIM = 128
BLOCK = 128
SPANS = 8

NT = (((1,), (1,)), ((), ()))
MESH = pl.DeviceIdType.MESH


def attend_block(q, do, k_cat, v_cat, kt_cat, vt_cat, factor):
    f32 = jnp.float32
    s = lax.dot_general(k_cat, q, NT, preferred_element_type=f32)
    dp = lax.dot_general(v_cat, do, NT, preferred_element_type=f32)
    top = jnp.max(s, axis=0, keepdims=True)
    e = jnp.exp((s - top) * factor)
    inv = 1.0 / jnp.sum(e, axis=0, keepdims=True)
    p = e * inv
    delta = jnp.sum(p * dp, axis=0, keepdims=True)
    pb = p.astype(jnp.bfloat16)
    ds = (p * (dp - delta)).astype(jnp.bfloat16)
    attn_t = jnp.dot(vt_cat, pb, preferred_element_type=f32)
    dq_t = jnp.dot(kt_cat, ds, preferred_element_type=f32) * factor
    return attn_t.T.astype(jnp.bfloat16), dq_t.T.astype(jnp.bfloat16), pb, ds


def fused_kernel(
    blks, columns, parts, unroll, factor,
    seg_ref, spans_ref, slot_ref, q_in, do_in, k_in, v_in,
    at_out, dq_out, dk_out, dv_out,
    q_s, do_s, k_s, v_s, kn, vn, kt, vt, p_s, ds_s, at_s, dq_s, dk_s, dv_s,
    in_send, out_send, k_recv, v_recv, q_recv, do_recv, out_recv,
):
    count = blks * columns
    near = blks // parts
    members = near * columns
    each = HEADS // members
    docs = blks
    blk, col = lax.axis_index("blk"), lax.axis_index("head")
    part, spot = blk // near, lax.rem(blk, near)
    mine = spot * columns + col
    bf16 = jnp.bfloat16

    def cols(index):
        return pl.ds(pl.multiple_of(index * HEAD_DIM, HEAD_DIM), HEAD_DIM)

    def member(m):
        return part * near + m // columns, lax.rem(m, columns)

    def doc_head(b, h):
        return lax.rem(b, near) * each + h

    def cad_head(m, h):
        return lax.rem(m, columns) * (HEADS // columns) + m // columns * each + h

    def local(src, dst, sem):
        pltpu.make_async_copy(src, dst, sem).start()

    def remote(src, dst, send, recv, where):
        pltpu.make_async_remote_copy(
            src_ref=src, dst_ref=dst, send_sem=send, recv_sem=recv,
            device_id=where, device_id_type=MESH,
        ).start()

    barrier = pltpu.get_barrier_semaphore()

    @pl.loop(1, count)
    def _(t):
        to = lax.rem(blk * columns + col + t, count)
        where = (to // columns, lax.rem(to, columns))
        pl.semaphore_signal(barrier, inc=1, device_id=where, device_id_type=MESH)

    for h in range(each):
        doc, cad = doc_head(blk, h), cad_head(mine, h)
        local(k_in.at[:, cols(doc)], k_s.at[h * docs + blk], k_recv.at[h])
        local(v_in.at[:, cols(doc)], v_s.at[h * docs + blk], v_recv.at[h])
        at = h * members + mine
        local(q_in.at[:, cols(cad)], q_s.at[at], q_recv.at[at])
        local(do_in.at[:, cols(cad)], do_s.at[at], do_recv.at[at])
    pl.semaphore_wait(barrier, count - 1)

    @pl.loop(0, each)
    def _(h):
        @pl.loop(1, blks)
        def _(t):
            to = lax.rem(blk + t, blks)
            doc = cols(doc_head(to, h))
            slot = h * docs + blk
            remote(k_in.at[:, doc], k_s.at[slot], in_send.at[0], k_recv.at[h], (to, col))
            remote(v_in.at[:, doc], v_s.at[slot], in_send.at[1], v_recv.at[h], (to, col))

        @pl.loop(1, members)
        def _(t):
            m = lax.rem(mine + t, members)
            cad = cols(cad_head(m, h))
            slot = h * members + mine
            remote(q_in.at[:, cad], q_s.at[slot], in_send.at[2], q_recv.at[slot], member(m))
            remote(do_in.at[:, cad], do_s.at[slot], in_send.at[3], do_recv.at[slot], member(m))

    @pl.loop(0, members)
    def _(m):
        p_s[m, SPANS] = jnp.zeros((BLOCK, BLOCK), bf16)
        ds_s[m, SPANS] = jnp.zeros((BLOCK, BLOCK), bf16)

    def wait_for(view, sem):
        pltpu.make_async_copy(view, view, sem).wait()

    def source(t):
        return lax.rem(mine + members - t, members)

    pair, chunk = 2, 8

    @pl.loop(0, each)
    def _(h):
        wait_for(k_s.at[pl.ds(h * docs, docs)], k_recv.at[h])
        wait_for(v_s.at[pl.ds(h * docs, docs)], v_recv.at[h])

        @pl.loop(0, docs)
        def _(d):
            k_tile, v_tile = k_s[h * docs + d], v_s[h * docs + d]
            kn[d] = k_tile
            vn[d] = v_tile
            kt[d] = k_tile.T
            vt[d] = v_tile.T

        here = cols(cad_head(mine, h))
        there = cols(doc_head(blk, h))

        def send_rows(t):
            m = source(t)
            slot = h * members + m

            @pl.when(t == 0)
            def _():
                local(at_s.at[slot], at_out.at[:, here], out_recv.at[0])
                local(dq_s.at[slot], dq_out.at[:, here], out_recv.at[1])

            @pl.when(t > 0)
            def _():
                remote(at_s.at[slot], at_out.at[:, here], out_send.at[0], out_recv.at[0], member(m))
                remote(dq_s.at[slot], dq_out.at[:, here], out_send.at[1], out_recv.at[1], member(m))

        @pl.loop(0, members // unroll)
        def _(step):
            @pl.when(step > 0)
            def _():
                for u in range(unroll):
                    send_rows((step - 1) * unroll + u)

            for u in range(unroll):
                slot = h * members + source(step * unroll + u)
                wait_for(q_s.at[slot], q_recv.at[slot])
                wait_for(do_s.at[slot], do_recv.at[slot])
            results = []
            for u in range(unroll):
                m = source(step * unroll + u)
                slot = h * members + m
                seg = seg_ref[part * members + m]
                ids = [spans_ref[seg, j] for j in range(SPANS)]
                k_cat = jnp.concatenate([kn[i] for i in ids], axis=0)
                v_cat = jnp.concatenate([vn[i] for i in ids], axis=0)
                kt_cat = jnp.concatenate([kt[i] for i in ids], axis=1)
                vt_cat = jnp.concatenate([vt[i] for i in ids], axis=1)
                q, do = q_s[slot], do_s[slot]
                results.append((m, slot, attend_block(q, do, k_cat, v_cat, kt_cat, vt_cat, factor)))
            for m, slot, (at, dq, pb, ds) in results:
                at_s[slot] = at
                dq_s[slot] = dq
                p_s[m, 0:SPANS] = pb.reshape(SPANS, BLOCK, BLOCK)
                ds_s[m, 0:SPANS] = ds.reshape(SPANS, BLOCK, BLOCK)

        for u in range(unroll):
            send_rows(members - unroll + u)

        def send_doc(t):
            to = lax.rem(blk + t, blks)
            slot = h * docs + to
            dk_to, dv_to = dk_out.at[part, :, there], dv_out.at[part, :, there]

            @pl.when(t == 0)
            def _():
                local(dk_s.at[slot], dk_to, out_recv.at[2])
                local(dv_s.at[slot], dv_to, out_recv.at[3])

            @pl.when(t > 0)
            def _():
                remote(dk_s.at[slot], dk_to, out_send.at[2], out_recv.at[2], (to, col))
                remote(dv_s.at[slot], dv_to, out_send.at[3], out_recv.at[3], (to, col))

        @pl.loop(0, docs // pair)
        def _(step):
            @pl.when(step > 0)
            def _():
                for u in range(pair):
                    send_doc((step - 1) * pair + u)

            to = [lax.rem(blk + step * pair + u, blks) for u in range(pair)]
            for held, right, out, scale in ((ds_s, q_s, dk_s, factor), (p_s, do_s, dv_s, None)):
                total = jnp.zeros((pair * BLOCK, HEAD_DIM), jnp.float32)
                for i in range(0, members, chunk):
                    segs = [seg_ref[part * members + i + c] for c in range(chunk)]
                    left = jnp.concatenate([
                        jnp.concatenate([held[i + c, slot_ref[segs[c], d]] for c in range(chunk)], axis=1)
                        for d in to], axis=0)
                    rows = right[pl.ds(h * members + i, chunk)].reshape(chunk * BLOCK, HEAD_DIM)
                    total = total + jnp.dot(left, rows, preferred_element_type=jnp.float32)
                if scale is not None:
                    total = total * scale
                for u, d in enumerate(to):
                    out[h * docs + d] = total[u * BLOCK:(u + 1) * BLOCK].astype(bf16)

        for u in range(pair):
            send_doc(docs - pair + u)

    def drain(array, blocks, sem):
        wait_for(array.at[pl.ds(0, blocks)], sem)

    for i, array in enumerate((k_s, v_s, q_s, do_s)):
        drain(array, each * ((blks if i < 2 else members) - 1), in_send.at[i])
    for i, array in enumerate((at_s, dq_s, dk_s, dv_s)):
        drain(array, each * ((members if i < 2 else blks) - 1), out_send.at[i])
    for i, array in enumerate((at_s, dq_s, dk_s, dv_s)):
        drain(array, each * (members if i < 2 else blks), out_recv.at[i])


def finish_kernel(at_in, dq_in, dk_in, dv_in, at_ref, dq_ref, dk_ref, dv_ref):
    at_ref[...] = at_in[...]
    dq_ref[...] = dq_in[...]
    for src, dst in ((dk_in, dk_ref), (dv_in, dv_ref)):
        total = src[0].astype(jnp.float32)
        for p in range(1, src.shape[0]):
            total = total + src[p].astype(jnp.float32)
        dst[...] = total.astype(jnp.bfloat16)


def finish(at, dq, dk, dv, steps=4):
    rows, wide = at.shape
    parts, docs, narrow = dk.shape
    cad = pl.BlockSpec((rows, wide // steps), lambda i: (0, i))
    partial = pl.BlockSpec((parts, docs, narrow // steps), lambda i: (0, 0, i))
    doc = pl.BlockSpec((docs, narrow // steps), lambda i: (0, i))
    return pl.pallas_call(
        finish_kernel,
        grid=(steps,),
        out_shape=[jax.ShapeDtypeStruct(a.shape[-2:], a.dtype) for a in (at, dq, dk, dv)],
        in_specs=[cad, cad, partial, partial],
        out_specs=[cad, cad, doc, doc],
        name="finish",
    )(at, dq, dk, dv)


def body(query, key, value, d_out, seg_map, spans):
    blks, columns = lax.axis_size("blk"), lax.axis_size("head")
    parts = 2
    docs = blks
    members = blks // parts * columns
    each = HEADS // members
    match = spans[:, :, None] == jnp.arange(docs, dtype=jnp.int32)
    place = jnp.arange(SPANS, dtype=jnp.int32)[None, :, None]
    slot = jnp.min(jnp.where(match, place, SPANS), axis=1)
    bf16 = jnp.bfloat16
    rows, tiles = (each * members, BLOCK, HEAD_DIM), (each * docs, BLOCK, HEAD_DIM)
    flipped = (docs, HEAD_DIM, BLOCK)
    held = (members, SPANS + 1, BLOCK, BLOCK)
    anywhere = pl.BlockSpec(memory_space=pl.ANY)
    scalars = pl.BlockSpec(memory_space=pltpu.SMEM)
    partial = jax.ShapeDtypeStruct((parts, *key.shape), bf16)
    cad = jax.ShapeDtypeStruct(query.shape, bf16)
    outs = pl.pallas_call(
        functools.partial(fused_kernel, blks, columns, parts, 2, 1.0 / math.sqrt(HEAD_DIM)),
        out_shape=[cad, cad, partial, partial],
        in_specs=[scalars] * 3 + [anywhere] * 4,
        out_specs=[anywhere] * 4,
        scratch_shapes=[
            pltpu.VMEM(rows, bf16), pltpu.VMEM(rows, bf16),
            pltpu.VMEM(tiles, bf16), pltpu.VMEM(tiles, bf16),
            pltpu.VMEM((docs, BLOCK, HEAD_DIM), bf16), pltpu.VMEM((docs, BLOCK, HEAD_DIM), bf16),
            pltpu.VMEM(flipped, bf16), pltpu.VMEM(flipped, bf16),
            pltpu.VMEM(held, bf16), pltpu.VMEM(held, bf16),
            pltpu.VMEM(rows, bf16), pltpu.VMEM(rows, bf16),
            pltpu.VMEM(tiles, bf16), pltpu.VMEM(tiles, bf16),
            pltpu.SemaphoreType.DMA((4,)), pltpu.SemaphoreType.DMA((4,)),
            pltpu.SemaphoreType.DMA((each,)), pltpu.SemaphoreType.DMA((each,)),
            pltpu.SemaphoreType.DMA((each * members,)), pltpu.SemaphoreType.DMA((each * members,)),
            pltpu.SemaphoreType.DMA((4,)),
        ],
        compiler_params=pltpu.CompilerParams(
            collective_id=0, has_side_effects=True, vmem_limit_bytes=60 << 20
        ),
        name="attend",
    )(seg_map, spans, slot, query, d_out, key, value)
    return finish(*outs)


def fits_one_head_each(mesh):
    return mesh.shape["blk"] * mesh.shape["head"] == HEADS


def head_pass(q_head, dout_head, key_head, value_head, id_groups):
    factor = 1.0 / math.sqrt(HEAD_DIM)
    group_width = q_head.shape[1]
    doc_blocks = key_head.shape[0]

    def one_group(sums, inputs):
        q_group, dout_group, group_ids = inputs
        flat_ids = group_ids.reshape(group_width * SPANS)
        key_tiles = jnp.take(key_head, flat_ids, axis=0).reshape(
            group_width, SPANS * BLOCK, HEAD_DIM
        )
        value_tiles = jnp.take(value_head, flat_ids, axis=0).reshape(
            group_width, SPANS * BLOCK, HEAD_DIM
        )
        scores = (
            jnp.einsum("cqd,ckd->cqk", q_group, key_tiles, preferred_element_type=jnp.float32)
            * factor
        )
        top_score = jnp.max(scores, axis=-1, keepdims=True)
        expo = jnp.exp(scores - top_score)
        prob = expo / jnp.sum(expo, axis=-1, keepdims=True)
        prob_b = prob.astype(jnp.bfloat16)
        attn = jnp.einsum("cqk,ckd->cqd", prob_b, value_tiles, preferred_element_type=jnp.float32)
        delta = jnp.sum(dout_group.astype(jnp.float32) * attn, axis=-1, keepdims=True)
        dprob = jnp.einsum(
            "cqd,ckd->cqk", dout_group, value_tiles, preferred_element_type=jnp.float32
        )
        dscore_b = (prob * (dprob - delta)).astype(jnp.bfloat16)
        grad_query = (
            jnp.einsum("cqk,ckd->cqd", dscore_b, key_tiles, preferred_element_type=jnp.float32)
            * factor
        ).astype(jnp.bfloat16)
        key_slots = (
            jnp.einsum("cqk,cqd->ckd", dscore_b, q_group, preferred_element_type=jnp.float32)
            * factor
        )
        value_slots = jnp.einsum(
            "cqk,cqd->ckd", prob_b, dout_group, preferred_element_type=jnp.float32
        )
        one_hot = (jnp.arange(doc_blocks, dtype=jnp.int32)[:, None] == flat_ids[None, :]).astype(
            jnp.float32
        )
        key_sums = sums[0] + jnp.dot(
            one_hot,
            key_slots.reshape(group_width * SPANS, BLOCK * HEAD_DIM),
            precision=lax.Precision.HIGHEST,
            preferred_element_type=jnp.float32,
        )
        value_sums = sums[1] + jnp.dot(
            one_hot,
            value_slots.reshape(group_width * SPANS, BLOCK * HEAD_DIM),
            precision=lax.Precision.HIGHEST,
            preferred_element_type=jnp.float32,
        )
        return ((key_sums, value_sums), (attn.astype(jnp.bfloat16), grad_query))

    zero_sums = jnp.zeros((doc_blocks, BLOCK * HEAD_DIM), jnp.float32)
    (key_sums, value_sums), (attn_head, grad_head) = lax.scan(
        one_group, (zero_sums, zero_sums), (q_head, dout_head, id_groups)
    )
    return (attn_head, grad_head, key_sums, value_sums)


def block_table(global_blocks, seg_map, spans):
    block_count = global_blocks.shape[0]
    seg_match = (
        global_blocks[:, None] == jnp.arange(seg_map.shape[0], dtype=jnp.int32)[None, :]
    ).astype(jnp.int32)
    seg_here = jnp.sum(seg_match * seg_map[None, :], axis=1)
    span_match = (seg_here[:, None] == jnp.arange(spans.shape[0], dtype=jnp.int32)[None, :]).astype(
        jnp.int32
    )
    block_ids = jnp.sum(span_match[:, :, None] * spans[None, :, :], axis=1)
    group_width = math.gcd(block_count, max(1, 512 // BLOCK))
    group_count = block_count // group_width
    return (block_ids.reshape(group_count, group_width, SPANS), group_count, group_width)


def by_heads(array, heads_count, group_count, group_width):
    block_count = group_count * group_width
    shaped = array.reshape(block_count, BLOCK, heads_count, HEAD_DIM).transpose(2, 0, 1, 3)
    return shaped.reshape(heads_count, group_count, group_width, BLOCK, HEAD_DIM)


def from_heads(array, heads_count):
    row_count = array.shape[1] * array.shape[2] * BLOCK
    shaped = array.reshape(heads_count, row_count, HEAD_DIM).transpose(1, 0, 2)
    return shaped.reshape(row_count, heads_count * HEAD_DIM)


def from_head_sums(array, heads_count):
    doc_rows = array.shape[1] // HEAD_DIM * BLOCK // BLOCK * array.shape[0] // array.shape[0]
    doc_rows = array.shape[1] * array.shape[2] // (BLOCK * HEAD_DIM) * BLOCK
    shaped = array.reshape(heads_count, doc_rows, HEAD_DIM).transpose(1, 0, 2)
    return shaped.reshape(doc_rows, heads_count * HEAD_DIM)


def body_shared(query, key, value, d_out, seg_map, spans):
    dummy_carry = jnp.zeros((), jnp.int32)
    heads_here = HEADS // lax.axis_size("blk")
    q_rows, dout_rows = (
        lax.all_to_all(query, "blk", split_axis=1, concat_axis=0, tiled=True),
        lax.all_to_all(d_out, "blk", split_axis=1, concat_axis=0, tiled=True),
    )
    per_device = query.shape[0] // BLOCK
    block_count = q_rows.shape[0] // BLOCK
    local_blocks = jnp.arange(block_count, dtype=jnp.int32)
    global_blocks = (
        local_blocks // per_device * lax.axis_size("head") + lax.axis_index("head")
    ) * per_device + local_blocks % per_device
    id_groups, group_count, group_width = block_table(global_blocks, seg_map, spans)
    q_heads = by_heads(q_rows, heads_here, group_count, group_width)
    dout_heads = by_heads(dout_rows, heads_here, group_count, group_width)
    key_wide, value_wide = (
        lax.all_gather(key, "head", axis=1, tiled=True),
        lax.all_gather(value, "head", axis=1, tiled=True),
    )
    key_cols, value_cols = (
        lax.all_to_all(key_wide, "blk", split_axis=1, concat_axis=0, tiled=True),
        lax.all_to_all(value_wide, "blk", split_axis=1, concat_axis=0, tiled=True),
    )
    doc_blocks = key_cols.shape[0] // BLOCK

    def to_blocks(array):
        return array.reshape(doc_blocks, BLOCK, heads_here, HEAD_DIM).transpose(2, 0, 1, 3)

    def scan_head(carry, inputs):
        q_head, dout_head, key_head, value_head = inputs
        return (carry, head_pass(q_head, dout_head, key_head, value_head, id_groups))

    _, (attn_heads, grad_heads, key_parts, value_parts) = lax.scan(
        scan_head, dummy_carry, (q_heads, dout_heads, to_blocks(key_cols), to_blocks(value_cols))
    )
    key_back, value_back = (
        lax.all_to_all(
            from_head_sums(key_parts, heads_here).astype(jnp.bfloat16),
            "blk",
            split_axis=0,
            concat_axis=1,
            tiled=True,
        ).astype(jnp.float32),
        lax.all_to_all(
            from_head_sums(value_parts, heads_here).astype(jnp.bfloat16),
            "blk",
            split_axis=0,
            concat_axis=1,
            tiled=True,
        ).astype(jnp.float32),
    )
    key_total, value_total = (
        lax.psum_scatter(
            key_back.astype(jnp.bfloat16), "head", scatter_dimension=1, tiled=True
        ).astype(jnp.float32),
        lax.psum_scatter(
            value_back.astype(jnp.bfloat16), "head", scatter_dimension=1, tiled=True
        ).astype(jnp.float32),
    )
    attn_out, d_query = (
        lax.all_to_all(
            from_heads(attn_heads, heads_here), "blk", split_axis=0, concat_axis=1, tiled=True
        ),
        lax.all_to_all(
            from_heads(grad_heads, heads_here), "blk", split_axis=0, concat_axis=1, tiled=True
        ),
    )
    return (attn_out, d_query, key_total.astype(jnp.bfloat16), value_total.astype(jnp.bfloat16))


def solution(mesh):
    placed = (
        P(("blk", "head"), None),
        P("blk", "head"),
        P("blk", "head"),
        P(("blk", "head"), None),
        P(),
        P(),
    )
    return jax.shard_map(
        body if fits_one_head_each(mesh) else body_shared,
        mesh=mesh,
        in_specs=placed,
        out_specs=(
            P(("blk", "head"), None),
            P(("blk", "head"), None),
            P("blk", "head"),
            P("blk", "head"),
        ),
        check_vma=False,
    )
```

```python
import functools
import math

import jax
import jax.numpy as jnp
from jax import lax
from jax.experimental import pallas as pl
from jax.experimental.pallas import tpu as pltpu
from jax.sharding import PartitionSpec as P

HEADS = 32
HEAD_DIM = 128
BLOCK = 128
SPANS = 8

NT = (((1,), (1,)), ((), ()))
MESH = pl.DeviceIdType.MESH


def attend_block(q, do, k_cat, v_cat, kt_cat, vt_cat, factor):
    f32 = jnp.float32
    s = lax.dot_general(k_cat, q, NT, preferred_element_type=f32)
    dp = lax.dot_general(v_cat, do, NT, preferred_element_type=f32)
    top = jnp.max(s, axis=0, keepdims=True)
    e = jnp.exp((s - top) * factor)
    inv = 1.0 / jnp.sum(e, axis=0, keepdims=True)
    p = e * inv
    delta = jnp.sum(p * dp, axis=0, keepdims=True)
    pb = p.astype(jnp.bfloat16)
    ds = (p * (dp - delta)).astype(jnp.bfloat16)
    attn_t = jnp.dot(vt_cat, pb, preferred_element_type=f32)
    dq_t = jnp.dot(kt_cat, ds, preferred_element_type=f32) * factor
    return attn_t.T.astype(jnp.bfloat16), dq_t.T.astype(jnp.bfloat16), pb, ds


def fused_kernel(
    blks, columns, parts, unroll, factor,
    seg_ref, spans_ref, q_in, do_in, k_in, v_in,
    at_out, dq_out, dk_out, dv_out,
    q_s, do_s, k_s, v_s, kn, vn, kt, vt, p_s, ds_s, at_s, dq_s, dk_s, dv_s,
    slot_ref, in_send, out_send, k_recv, v_recv, q_recv, do_recv, out_recv,
):
    count = blks * columns
    near = blks // parts
    members = near * columns
    each = HEADS // members
    docs = blks
    blk, col = lax.axis_index("blk"), lax.axis_index("head")
    part, spot = blk // near, lax.rem(blk, near)
    mine = spot * columns + col
    bf16 = jnp.bfloat16

    def cols(index):
        return pl.ds(pl.multiple_of(index * HEAD_DIM, HEAD_DIM), HEAD_DIM)

    def member(m):
        return part * near + m // columns, lax.rem(m, columns)

    def doc_head(b, h):
        return lax.rem(b, near) * each + h

    def cad_head(m, h):
        return lax.rem(m, columns) * (HEADS // columns) + m // columns * each + h

    def turn(t, size):
        half = (t + 1) // 2
        back = lax.rem(t + 1, 2)
        return lax.rem(half + back * (size - 2 * half) + size, size)

    def local(src, dst, sem):
        pltpu.make_async_copy(src, dst, sem).start()

    def remote(src, dst, send, recv, where):
        pltpu.make_async_remote_copy(
            src_ref=src, dst_ref=dst, send_sem=send, recv_sem=recv,
            device_id=where, device_id_type=MESH,
        ).start()

    barrier = pltpu.get_barrier_semaphore()

    @pl.loop(1, count)
    def _(t):
        to = lax.rem(blk * columns + col + t, count)
        where = (to // columns, lax.rem(to, columns))
        pl.semaphore_signal(barrier, inc=1, device_id=where, device_id_type=MESH)

    for h in range(each):
        doc, cad = doc_head(blk, h), cad_head(mine, h)
        local(k_in.at[:, cols(doc)], k_s.at[h * docs + blk], k_recv.at[h])
        local(v_in.at[:, cols(doc)], v_s.at[h * docs + blk], v_recv.at[h])
        at = h * members + mine
        local(q_in.at[:, cols(cad)], q_s.at[at], q_recv.at[at])
        local(do_in.at[:, cols(cad)], do_s.at[at], do_recv.at[at])
    pl.semaphore_wait(barrier, count - 1)

    @pl.loop(0, each)
    def _(h):
        @pl.loop(1, blks)
        def _(t):
            to = lax.rem(blk + turn(t, blks), blks)
            doc = cols(doc_head(to, h))
            slot = h * docs + blk
            remote(k_in.at[:, doc], k_s.at[slot], in_send.at[0], k_recv.at[h], (to, col))
            remote(v_in.at[:, doc], v_s.at[slot], in_send.at[1], v_recv.at[h], (to, col))

        @pl.loop(1, members)
        def _(t):
            m = lax.rem(mine + turn(t, members), members)
            cad = cols(cad_head(m, h))
            slot = h * members + mine
            remote(q_in.at[:, cad], q_s.at[slot], in_send.at[2], q_recv.at[slot], member(m))
            remote(do_in.at[:, cad], do_s.at[slot], in_send.at[3], do_recv.at[slot], member(m))

    @pl.loop(0, spans_ref.shape[0])
    def _(g):
        named = [spans_ref[g, j] for j in range(SPANS)]
        for d in range(docs):
            found = SPANS
            for j in range(SPANS):
                found = jnp.where(named[j] == d, j, found)
            slot_ref[g, d] = found

    @pl.loop(0, members)
    def _(m):
        p_s[m, SPANS] = jnp.zeros((BLOCK, BLOCK), bf16)
        ds_s[m, SPANS] = jnp.zeros((BLOCK, BLOCK), bf16)

    def wait_for(view, sem):
        pltpu.make_async_copy(view, view, sem).wait()

    def source(t):
        return lax.rem(mine + members - turn(t, members), members)

    pair, chunk = 2, 8

    @pl.loop(0, each)
    def _(h):
        wait_for(k_s.at[pl.ds(h * docs, docs)], k_recv.at[h])
        wait_for(v_s.at[pl.ds(h * docs, docs)], v_recv.at[h])

        @pl.loop(0, docs)
        def _(d):
            k_tile, v_tile = k_s[h * docs + d], v_s[h * docs + d]
            kn[d] = k_tile
            vn[d] = v_tile
            kt[d] = k_tile.T
            vt[d] = v_tile.T

        here = cols(cad_head(mine, h))
        there = cols(doc_head(blk, h))

        def send_rows(t):
            m = source(t)
            slot = h * members + m

            @pl.when(t == 0)
            def _():
                local(at_s.at[slot], at_out.at[:, here], out_recv.at[0])
                local(dq_s.at[slot], dq_out.at[:, here], out_recv.at[1])

            @pl.when(t > 0)
            def _():
                remote(at_s.at[slot], at_out.at[:, here], out_send.at[0], out_recv.at[0], member(m))
                remote(dq_s.at[slot], dq_out.at[:, here], out_send.at[1], out_recv.at[1], member(m))

        @pl.loop(0, members // unroll)
        def _(step):
            @pl.when(step > 0)
            def _():
                for u in range(unroll):
                    send_rows((step - 1) * unroll + u)

            for u in range(unroll):
                slot = h * members + source(step * unroll + u)
                wait_for(q_s.at[slot], q_recv.at[slot])
                wait_for(do_s.at[slot], do_recv.at[slot])
            results = []
            for u in range(unroll):
                m = source(step * unroll + u)
                slot = h * members + m
                seg = seg_ref[part * members + m]
                ids = [spans_ref[seg, j] for j in range(SPANS)]
                k_cat = jnp.concatenate([kn[i] for i in ids], axis=0)
                v_cat = jnp.concatenate([vn[i] for i in ids], axis=0)
                kt_cat = jnp.concatenate([kt[i] for i in ids], axis=1)
                vt_cat = jnp.concatenate([vt[i] for i in ids], axis=1)
                q, do = q_s[slot], do_s[slot]
                results.append((m, slot, attend_block(q, do, k_cat, v_cat, kt_cat, vt_cat, factor)))
            for m, slot, (at, dq, pb, ds) in results:
                at_s[slot] = at
                dq_s[slot] = dq
                p_s[m, 0:SPANS] = pb.reshape(SPANS, BLOCK, BLOCK)
                ds_s[m, 0:SPANS] = ds.reshape(SPANS, BLOCK, BLOCK)

        for u in range(unroll):
            send_rows(members - unroll + u)

        def send_doc(t):
            to = lax.rem(blk + turn(t, blks), blks)
            slot = h * docs + to
            dk_to, dv_to = dk_out.at[part, :, there], dv_out.at[part, :, there]

            @pl.when(t == 0)
            def _():
                local(dk_s.at[slot], dk_to, out_recv.at[2])
                local(dv_s.at[slot], dv_to, out_recv.at[3])

            @pl.when(t > 0)
            def _():
                remote(dk_s.at[slot], dk_to, out_send.at[2], out_recv.at[2], (to, col))
                remote(dv_s.at[slot], dv_to, out_send.at[3], out_recv.at[3], (to, col))

        @pl.loop(0, docs // pair)
        def _(step):
            @pl.when(step > 0)
            def _():
                for u in range(pair):
                    send_doc((step - 1) * pair + u)

            to = [lax.rem(blk + turn(step * pair + u, blks), blks) for u in range(pair)]
            for held, right, out, scale in ((ds_s, q_s, dk_s, factor), (p_s, do_s, dv_s, None)):
                total = jnp.zeros((pair * BLOCK, HEAD_DIM), jnp.float32)
                for i in range(0, members, chunk):
                    segs = [seg_ref[part * members + i + c] for c in range(chunk)]
                    left = jnp.concatenate([
                        jnp.concatenate([held[i + c, slot_ref[segs[c], d]] for c in range(chunk)], axis=1)
                        for d in to], axis=0)
                    rows = right[pl.ds(h * members + i, chunk)].reshape(chunk * BLOCK, HEAD_DIM)
                    total = total + jnp.dot(left, rows, preferred_element_type=jnp.float32)
                if scale is not None:
                    total = total * scale
                for u, d in enumerate(to):
                    out[h * docs + d] = total[u * BLOCK:(u + 1) * BLOCK].astype(bf16)

        for u in range(pair):
            send_doc(docs - pair + u)

    def drain(array, blocks, sem):
        wait_for(array.at[pl.ds(0, blocks)], sem)

    for i, array in enumerate((k_s, v_s, q_s, do_s)):
        drain(array, each * ((blks if i < 2 else members) - 1), in_send.at[i])
    for i, array in enumerate((at_s, dq_s, dk_s, dv_s)):
        drain(array, each * ((members if i < 2 else blks) - 1), out_send.at[i])
    for i, array in enumerate((at_s, dq_s, dk_s, dv_s)):
        drain(array, each * (members if i < 2 else blks), out_recv.at[i])


def finish_kernel(at_in, dq_in, dk_in, dv_in, at_ref, dq_ref, dk_ref, dv_ref):
    at_ref[...] = at_in[...]
    dq_ref[...] = dq_in[...]
    for src, dst in ((dk_in, dk_ref), (dv_in, dv_ref)):
        total = src[0].astype(jnp.float32)
        for p in range(1, src.shape[0]):
            total = total + src[p].astype(jnp.float32)
        dst[...] = total.astype(jnp.bfloat16)


def finish(at, dq, dk, dv, steps=2):
    rows, wide = at.shape
    parts, docs, narrow = dk.shape
    cad = pl.BlockSpec((rows, wide // steps), lambda i: (0, i))
    partial = pl.BlockSpec((parts, docs, narrow // steps), lambda i: (0, 0, i))
    doc = pl.BlockSpec((docs, narrow // steps), lambda i: (0, i))
    return pl.pallas_call(
        finish_kernel,
        grid=(steps,),
        out_shape=[jax.ShapeDtypeStruct(a.shape[-2:], a.dtype) for a in (at, dq, dk, dv)],
        in_specs=[cad, cad, partial, partial],
        out_specs=[cad, cad, doc, doc],
        name="finish",
    )(at, dq, dk, dv)


def body(query, key, value, d_out, seg_map, spans):
    if query.shape[0] != BLOCK or key.shape[0] != BLOCK:
        return body_shared(query, key, value, d_out, seg_map, spans)
    blks, columns = lax.axis_size("blk"), lax.axis_size("head")
    parts = 2
    docs = blks
    members = blks // parts * columns
    each = HEADS // members
    bf16 = jnp.bfloat16
    rows, tiles = (each * members, BLOCK, HEAD_DIM), (each * docs, BLOCK, HEAD_DIM)
    flipped = (docs, HEAD_DIM, BLOCK)
    held = (members, SPANS + 1, BLOCK, BLOCK)
    anywhere = pl.BlockSpec(memory_space=pl.ANY)
    scalars = pl.BlockSpec(memory_space=pltpu.SMEM)
    partial = jax.ShapeDtypeStruct((parts, *key.shape), bf16)
    cad = jax.ShapeDtypeStruct(query.shape, bf16)
    outs = pl.pallas_call(
        functools.partial(fused_kernel, blks, columns, parts, 2, 1.0 / math.sqrt(HEAD_DIM)),
        out_shape=[cad, cad, partial, partial],
        in_specs=[scalars] * 2 + [anywhere] * 4,
        out_specs=[anywhere] * 4,
        scratch_shapes=[
            pltpu.VMEM(rows, bf16), pltpu.VMEM(rows, bf16),
            pltpu.VMEM(tiles, bf16), pltpu.VMEM(tiles, bf16),
            pltpu.VMEM((docs, BLOCK, HEAD_DIM), bf16), pltpu.VMEM((docs, BLOCK, HEAD_DIM), bf16),
            pltpu.VMEM(flipped, bf16), pltpu.VMEM(flipped, bf16),
            pltpu.VMEM(held, bf16), pltpu.VMEM(held, bf16),
            pltpu.VMEM(rows, bf16), pltpu.VMEM(rows, bf16),
            pltpu.VMEM(tiles, bf16), pltpu.VMEM(tiles, bf16),
            pltpu.SMEM((spans.shape[0], docs), jnp.int32),
            pltpu.SemaphoreType.DMA((4,)), pltpu.SemaphoreType.DMA((4,)),
            pltpu.SemaphoreType.DMA((each,)), pltpu.SemaphoreType.DMA((each,)),
            pltpu.SemaphoreType.DMA((each * members,)), pltpu.SemaphoreType.DMA((each * members,)),
            pltpu.SemaphoreType.DMA((4,)),
        ],
        compiler_params=pltpu.CompilerParams(
            collective_id=0, has_side_effects=True, vmem_limit_bytes=60 << 20
        ),
        name="attend",
    )(seg_map, spans, query, d_out, key, value)
    return finish(*outs)


def fits_one_head_each(mesh):
    return mesh.shape["blk"] * mesh.shape["head"] == HEADS and mesh.shape["blk"] % 8 == 0


def head_pass(q_head, dout_head, key_head, value_head, id_groups):
    factor = 1.0 / math.sqrt(HEAD_DIM)
    group_width = q_head.shape[1]
    doc_blocks = key_head.shape[0]

    def one_group(sums, inputs):
        q_group, dout_group, group_ids = inputs
        flat_ids = group_ids.reshape(group_width * SPANS)
        key_tiles = jnp.take(key_head, flat_ids, axis=0).reshape(
            group_width, SPANS * BLOCK, HEAD_DIM
        )
        value_tiles = jnp.take(value_head, flat_ids, axis=0).reshape(
            group_width, SPANS * BLOCK, HEAD_DIM
        )
        scores = (
            jnp.einsum("cqd,ckd->cqk", q_group, key_tiles, preferred_element_type=jnp.float32)
            * factor
        )
        top_score = jnp.max(scores, axis=-1, keepdims=True)
        expo = jnp.exp(scores - top_score)
        prob = expo / jnp.sum(expo, axis=-1, keepdims=True)
        prob_b = prob.astype(jnp.bfloat16)
        attn = jnp.einsum("cqk,ckd->cqd", prob_b, value_tiles, preferred_element_type=jnp.float32)
        delta = jnp.sum(dout_group.astype(jnp.float32) * attn, axis=-1, keepdims=True)
        dprob = jnp.einsum(
            "cqd,ckd->cqk", dout_group, value_tiles, preferred_element_type=jnp.float32
        )
        dscore_b = (prob * (dprob - delta)).astype(jnp.bfloat16)
        grad_query = (
            jnp.einsum("cqk,ckd->cqd", dscore_b, key_tiles, preferred_element_type=jnp.float32)
            * factor
        ).astype(jnp.bfloat16)
        key_slots = (
            jnp.einsum("cqk,cqd->ckd", dscore_b, q_group, preferred_element_type=jnp.float32)
            * factor
        )
        value_slots = jnp.einsum(
            "cqk,cqd->ckd", prob_b, dout_group, preferred_element_type=jnp.float32
        )
        one_hot = (jnp.arange(doc_blocks, dtype=jnp.int32)[:, None] == flat_ids[None, :]).astype(
            jnp.float32
        )
        key_sums = sums[0] + jnp.dot(
            one_hot,
            key_slots.reshape(group_width * SPANS, BLOCK * HEAD_DIM),
            precision=lax.Precision.HIGHEST,
            preferred_element_type=jnp.float32,
        )
        value_sums = sums[1] + jnp.dot(
            one_hot,
            value_slots.reshape(group_width * SPANS, BLOCK * HEAD_DIM),
            precision=lax.Precision.HIGHEST,
            preferred_element_type=jnp.float32,
        )
        return ((key_sums, value_sums), (attn.astype(jnp.bfloat16), grad_query))

    zero_sums = jnp.zeros((doc_blocks, BLOCK * HEAD_DIM), jnp.float32)
    (key_sums, value_sums), (attn_head, grad_head) = lax.scan(
        one_group, (zero_sums, zero_sums), (q_head, dout_head, id_groups)
    )
    return (attn_head, grad_head, key_sums, value_sums)


def block_table(global_blocks, seg_map, spans):
    block_count = global_blocks.shape[0]
    seg_match = (
        global_blocks[:, None] == jnp.arange(seg_map.shape[0], dtype=jnp.int32)[None, :]
    ).astype(jnp.int32)
    seg_here = jnp.sum(seg_match * seg_map[None, :], axis=1)
    span_match = (seg_here[:, None] == jnp.arange(spans.shape[0], dtype=jnp.int32)[None, :]).astype(
        jnp.int32
    )
    block_ids = jnp.sum(span_match[:, :, None] * spans[None, :, :], axis=1)
    group_width = math.gcd(block_count, max(1, 512 // BLOCK))
    group_count = block_count // group_width
    return (block_ids.reshape(group_count, group_width, SPANS), group_count, group_width)


def by_heads(array, heads_count, group_count, group_width):
    block_count = group_count * group_width
    shaped = array.reshape(block_count, BLOCK, heads_count, HEAD_DIM).transpose(2, 0, 1, 3)
    return shaped.reshape(heads_count, group_count, group_width, BLOCK, HEAD_DIM)


def from_heads(array, heads_count):
    row_count = array.shape[1] * array.shape[2] * BLOCK
    shaped = array.reshape(heads_count, row_count, HEAD_DIM).transpose(1, 0, 2)
    return shaped.reshape(row_count, heads_count * HEAD_DIM)


def from_head_sums(array, heads_count):
    doc_rows = array.shape[1] // HEAD_DIM * BLOCK // BLOCK * array.shape[0] // array.shape[0]
    doc_rows = array.shape[1] * array.shape[2] // (BLOCK * HEAD_DIM) * BLOCK
    shaped = array.reshape(heads_count, doc_rows, HEAD_DIM).transpose(1, 0, 2)
    return shaped.reshape(doc_rows, heads_count * HEAD_DIM)


def body_shared(query, key, value, d_out, seg_map, spans):
    dummy_carry = jnp.zeros((), jnp.int32)
    heads_here = HEADS // lax.axis_size("blk")
    q_rows, dout_rows = (
        lax.all_to_all(query, "blk", split_axis=1, concat_axis=0, tiled=True),
        lax.all_to_all(d_out, "blk", split_axis=1, concat_axis=0, tiled=True),
    )
    per_device = query.shape[0] // BLOCK
    block_count = q_rows.shape[0] // BLOCK
    local_blocks = jnp.arange(block_count, dtype=jnp.int32)
    global_blocks = (
        local_blocks // per_device * lax.axis_size("head") + lax.axis_index("head")
    ) * per_device + local_blocks % per_device
    id_groups, group_count, group_width = block_table(global_blocks, seg_map, spans)
    q_heads = by_heads(q_rows, heads_here, group_count, group_width)
    dout_heads = by_heads(dout_rows, heads_here, group_count, group_width)
    key_wide, value_wide = (
        lax.all_gather(key, "head", axis=1, tiled=True),
        lax.all_gather(value, "head", axis=1, tiled=True),
    )
    key_cols, value_cols = (
        lax.all_to_all(key_wide, "blk", split_axis=1, concat_axis=0, tiled=True),
        lax.all_to_all(value_wide, "blk", split_axis=1, concat_axis=0, tiled=True),
    )
    doc_blocks = key_cols.shape[0] // BLOCK

    def to_blocks(array):
        return array.reshape(doc_blocks, BLOCK, heads_here, HEAD_DIM).transpose(2, 0, 1, 3)

    def scan_head(carry, inputs):
        q_head, dout_head, key_head, value_head = inputs
        return (carry, head_pass(q_head, dout_head, key_head, value_head, id_groups))

    _, (attn_heads, grad_heads, key_parts, value_parts) = lax.scan(
        scan_head, dummy_carry, (q_heads, dout_heads, to_blocks(key_cols), to_blocks(value_cols))
    )
    key_back, value_back = (
        lax.all_to_all(
            from_head_sums(key_parts, heads_here).astype(jnp.bfloat16),
            "blk",
            split_axis=0,
            concat_axis=1,
            tiled=True,
        ).astype(jnp.float32),
        lax.all_to_all(
            from_head_sums(value_parts, heads_here).astype(jnp.bfloat16),
            "blk",
            split_axis=0,
            concat_axis=1,
            tiled=True,
        ).astype(jnp.float32),
    )
    key_total, value_total = (
        lax.psum_scatter(
            key_back.astype(jnp.bfloat16), "head", scatter_dimension=1, tiled=True
        ).astype(jnp.float32),
        lax.psum_scatter(
            value_back.astype(jnp.bfloat16), "head", scatter_dimension=1, tiled=True
        ).astype(jnp.float32),
    )
    attn_out, d_query = (
        lax.all_to_all(
            from_heads(attn_heads, heads_here), "blk", split_axis=0, concat_axis=1, tiled=True
        ),
        lax.all_to_all(
            from_heads(grad_heads, heads_here), "blk", split_axis=0, concat_axis=1, tiled=True
        ),
    )
    return (attn_out, d_query, key_total.astype(jnp.bfloat16), value_total.astype(jnp.bfloat16))


def solution(mesh):
    placed = (
        P(("blk", "head"), None),
        P("blk", "head"),
        P("blk", "head"),
        P(("blk", "head"), None),
        P(),
        P(),
    )
    return jax.shard_map(
        body if fits_one_head_each(mesh) else body_shared,
        mesh=mesh,
        in_specs=placed,
        out_specs=(
            P(("blk", "head"), None),
            P(("blk", "head"), None),
            P("blk", "head"),
            P("blk", "head"),
        ),
        check_vma=False,
    )
```
